1024 devices in a mesh: row: 64 (over x, y), col: 16 (over z, core).
Axes of the slice: x: 8, y: 8, z: 8, core: 2. Of those that a mesh axis runs over, the one named last changes fastest.
Arguments:
- x_tiles: bfloat16 [1024, 8, 256, 256], P(('row', 'col')), as said below
- columns: int32 [1024, 8], P(('row', 'col')), may hold values from 0 to 1023, as said below
- branch: int32 [64, 2], P('row'), may hold values from 0 to 1
Outputs:
- purified: float32 [1024, 8, 256, 256], P(('row', 'col'))
- occupation: float32 [64], P('row')
The draws below stay inside these ranges and needn't reach their ends.
Inputs may be any that keep to these rules, and one draw needn't show every extreme that they name: `columns`: block rows form fragments of 16 consecutive rows, each with two halves of 8 rows. Slot 0 of a block row is the row itself; its other slots hold, in ascending order, every row of the other half of its fragment but one, so that the pattern is symmetric and no two rows of one half are coupled. `x_tiles`: every tile of the pattern is the transpose of its mirror tile, and diagonal tiles are symmetric.
All inputs are finite; a program needn't handle non-finite values.
Results may differ from the reference program's by a relative error of at most 0.0028.
Values may be sent and summed in bfloat16 or wider, within the bound.
No kernel may reach another device: no remote copies, remote signals or barrier semaphores. Data moves between devices by JAX's collectives and lax.ppermute only.
A program may use at most 32 MiB of HBM per device.

```python
import jax
import jax.numpy as jnp
from jax import lax

TS = 256
TPR = 8
CLUSTER = 16
STEPS = 2
NB = 1024
FRAGMENTS = 64


def pattern_parts(key):
    clusters = NB // CLUSTER
    half_rows = CLUSTER // 2
    cluster_keys = jax.random.split(jax.random.fold_in(key, 11), clusters)
    orderings = jax.vmap(lambda subkey: jax.random.permutation(subkey, half_rows))(cluster_keys).astype(jnp.int32)
    inverse = jnp.argsort(orderings, axis=1).astype(jnp.int32)
    offsets = jnp.arange(half_rows - 1, dtype=jnp.int32)
    upper_rows = half_rows + offsets[None, None, :] + (offsets[None, None, :] >= orderings[:, :, None]).astype(jnp.int32)
    lower_rows = offsets[None, None, :] + (offsets[None, None, :] >= inverse[:, :, None]).astype(jnp.int32)
    partners = jnp.concatenate([upper_rows, lower_rows], axis=1)
    itself = jnp.broadcast_to(jnp.arange(CLUSTER, dtype=jnp.int32)[None, :, None], (clusters, CLUSTER, 1))
    local_cols = jnp.concatenate([itself, partners], axis=2)
    row_base = (jnp.arange(clusters, dtype=jnp.int32) * CLUSTER)[:, None, None]
    return ((local_cols + row_base).reshape(NB, TPR), lower_rows, orderings)


def draw_columns(key, part):
    return pattern_parts(key)[0]


def draw_x_tiles(key, part):
    clusters = NB // CLUSTER
    half_rows = CLUSTER // 2
    unused, lower_rows, orderings = pattern_parts(key)
    sample_key = jax.random.fold_in(key, 3)
    samples = jax.random.normal(sample_key, (clusters, CLUSTER, TPR, TS, TS), jnp.float32)
    spread = 0.9 / (TS * TPR) ** 0.5
    diagonal = (samples[:, :, 0] + jnp.swapaxes(samples[:, :, 0], 2, 3)) * (spread / 2.0 ** 0.5)
    first_half = samples[:, :half_rows]
    upper_tiles = first_half[:, :, 1:] * spread
    row_ids = jnp.arange(half_rows, dtype=jnp.int32)[None, :, None]
    order_at = jax.vmap(lambda order, index_set: order[index_set])(orderings, lower_rows)
    slot_ids = 1 + row_ids - (row_ids > order_at).astype(jnp.int32)
    picked = jax.vmap(lambda block, index_set, slot_set: block[index_set, slot_set])(first_half, lower_rows, slot_ids)
    lower_tiles = jnp.swapaxes(picked, 3, 4) * spread
    upper_block = jnp.concatenate([diagonal[:, :half_rows, None], upper_tiles], axis=2)
    lower_block = jnp.concatenate([diagonal[:, half_rows:, None], lower_tiles], axis=2)
    return jnp.concatenate([upper_block, lower_block], axis=1).reshape(NB, TPR, TS, TS).astype(jnp.bfloat16)


def touch_ends(array, own_key, least, top_value):
    dims = array.shape
    index_at = [jax.random.randint(jax.random.fold_in(own_key, axis), (), 0, dims[axis]) for axis in range(len(dims))]
    array = array.at[tuple(index_at)].set(least)
    longest = dims.index(max(dims))
    index_at[longest] = (index_at[longest] + 1) % dims[longest]
    return array.at[tuple(index_at)].set(top_value)


def setup_inputs(seed: int = 0) -> dict:
    arg_keys = jax.random.split(jax.random.key(seed), 4)
    x_tiles = draw_x_tiles(jax.random.fold_in(arg_keys[3], 71), 0)
    columns = draw_columns(jax.random.fold_in(arg_keys[3], 71), 0)
    branch = touch_ends(jax.random.randint(arg_keys[2], (FRAGMENTS, STEPS), 0, 2), jax.random.fold_in(arg_keys[2], 1), 0, 1).astype(jnp.int32)
    return {"x_tiles": x_tiles, "columns": columns, "branch": branch}


def advance(tiles_in, cols_in, step_sign):
    tile_size = tiles_in.shape[-1]
    row_count = tiles_in.shape[0]
    rounded = tiles_in.astype(jnp.bfloat16).astype(jnp.float32)
    diagonal = rounded[:, 0]
    diagonal_sum = jnp.einsum("ctij,ctkj->cik", rounded, rounded, precision=lax.Precision.HIGHEST)
    local_term = jnp.einsum("cij,csjk->csik", diagonal, rounded[:, 1:], precision=lax.Precision.HIGHEST)
    partner = cols_in[:, 1:]
    matches = cols_in[partner] == jnp.arange(row_count, dtype=jnp.int32)[:, None, None]
    back_slot = jnp.argmax(matches, axis=2).astype(jnp.int32) - 1
    mirrored = local_term[partner, back_slot]
    partner_term = lax.optimization_barrier(jnp.swapaxes(mirrored, 2, 3).astype(jnp.bfloat16)).astype(jnp.float32)
    identity = jnp.eye(tile_size, dtype=jnp.float32)
    new_diagonal = tiles_in[:, 0] + step_sign * (diagonal_sum - 0.25 * identity)
    new_others = tiles_in[:, 1:] + step_sign * (local_term + partner_term)
    return jnp.concatenate([new_diagonal[:, None], new_others], axis=1)


def reference(x_tiles, columns, branch):
    clusters = NB // CLUSTER
    tiles = x_tiles.astype(jnp.float32).reshape(clusters, CLUSTER, TPR, TS, TS)
    local_cols = (columns % CLUSTER).astype(jnp.int32).reshape(clusters, CLUSTER, TPR)
    signs = (2 * branch - 1).astype(jnp.float32)

    def purify(inputs):
        current, cols_in, sign_row = inputs
        for iteration in range(STEPS):
            current = advance(current, cols_in, sign_row[iteration])
        trace_sum = jnp.sum(jnp.diagonal(current[:, 0], axis1=1, axis2=2))
        return current, trace_sum / (CLUSTER * TS) + 0.5

    purified, occupation = lax.map(purify, (tiles, local_cols, signs))
    return purified.reshape(NB, TPR, TS, TS), occupation
```

```python
import jax
import jax.numpy as jnp
from jax import lax
from jax.experimental import pallas as pl
from jax.experimental.pallas import tpu as pltpu
from jax.sharding import PartitionSpec as P

BF = jnp.bfloat16
F32 = jnp.float32
SIDE_ROWS = 8


def nt(a, b):
    return lax.dot_general(a, b, (((1,), (1,)), ((), ())), preferred_element_type=F32)


def nn(a, b):
    return jnp.dot(a, b, preferred_element_type=F32)


def index_grids(h):
    return (lax.broadcasted_iota(jnp.int32, (h, h), 0), lax.broadcasted_iota(jnp.int32, (h, h), 1))


def quarter_identity(size):
    row, col = index_grids(size)
    return jnp.where(row == col, 0.25, 0.0).astype(F32)


def sign_of(branch_ref, step):
    return (2 * branch_ref[0, step] - 1).astype(F32)


def folded(tile):
    h = tile.shape[0] // 2
    row, col = index_grids(h)
    first, second = tile[:h, :h], tile[h:, h:]
    mixed = jnp.where(row <= col, first, second)
    second_diag = jnp.sum(jnp.where(row == col, second, 0.0), axis=0, keepdims=True)
    return mixed, tile[:h, h:], second_diag


def unfolded(mixed, corner, second_diag, grids):
    row, col = grids
    low = jnp.where(row > col, mixed, 0.0)
    zero = jnp.zeros_like(low)
    stack = lambda a, b, c, d: jnp.concatenate(
        [jnp.concatenate([a, b], axis=1), jnp.concatenate([c, d], axis=1)], axis=0
    ).astype(BF)
    straight = stack(jnp.where(row <= col, mixed, 0.0), corner, zero, jnp.where(row == col, second_diag, low))
    flipped = stack(jnp.where(row < col, mixed, 0.0), corner, zero, low)
    return straight, flipped


def partner_product(tile, index, gathered_ref, side_ref, rows_ref, grids, diag_row, tail_rows):
    h = gathered_ref.shape[2]
    rows_ref[: gathered_ref.shape[1]] = gathered_ref[index].astype(F32)
    side = side_ref[index].astype(F32)
    for k, where in enumerate(tail_rows):
        at = 2 * h - len(tail_rows) + k
        rows_ref[at : at + 1] = side[where : where + 1]
    straight, flipped = unfolded(rows_ref[:h], rows_ref[h:], side[diag_row : diag_row + 1], grids)
    return (nn(tile, straight) + nt(tile, flipped)).astype(BF).astype(F32)


def first_kernel(branch_ref, x_hbm, sent0_ref, side_ref, sent1_ref, diag_ref, x_ref, sems):
    tiles, size = x_ref.shape[:2]
    h = size // 2
    loads = [pltpu.make_async_copy(x_hbm.at[s], x_ref.at[s], sems.at[s]) for s in range(tiles)]
    for load in loads:
        load.start()
    sign = sign_of(branch_ref, 0)
    loads[0].wait()
    x0 = x_ref[0]
    old = x0.astype(F32)
    mixed0, corner0, diag0 = folded(old)
    sent0_ref[0, :h] = mixed0.astype(BF)
    sent0_ref[0, h:] = corner0[: h - 1].astype(BF)
    total = nt(x0, x0)
    for slot in range(1, tiles):
        loads[slot].wait()
        total += nt(x_ref[slot], x_ref[slot])
    new = old + sign * (total - quarter_identity(size))
    diag_ref[...] = new
    mixed1, corner1, diag1 = folded(new)
    sent1_ref[:h] = mixed1.astype(BF)
    sent1_ref[h:] = corner1[: h - 1].astype(BF)
    at = lax.broadcasted_iota(jnp.int32, (SIDE_ROWS, h), 0)
    side = jnp.zeros((SIDE_ROWS, h), F32)
    for k, line in enumerate((diag0, corner0[h - 1 :], diag1, corner1[h - 2 : h - 1], corner1[h - 1 :])):
        side = jnp.where(at == k, line, side)
    for slot in range(side_ref.shape[0]):
        side_ref[slot] = side.astype(BF)


def second_kernel(
    cluster, branch_ref, cols_ref, x_hbm, diag_ref, held_ref, gathered_ref, side_ref,
    new_hbm, sent_ref, x_ref, new_ref, rows_ref, load_sems, store_sems,
):
    tiles, size = x_ref.shape[:2]
    h = size // 2
    loads = [pltpu.make_async_copy(x_hbm.at[s], x_ref.at[s], load_sems.at[s]) for s in range(tiles)]
    stores = [pltpu.make_async_copy(new_ref.at[s], new_hbm.at[s], store_sems.at[s]) for s in range(tiles - 1)]
    for load in loads:
        load.start()
    sign, next_sign = sign_of(branch_ref, 0), sign_of(branch_ref, 1)
    grids = index_grids(h)
    diag = diag_ref[...]
    rounded = diag.astype(BF).astype(F32)
    squares = rounded * rounded
    loads[0].wait()
    x0 = x_ref[0]
    for slot in range(1, tiles):
        loads[slot].wait()
        tile = x_ref[slot]
        index = lax.rem(cols_ref[0, slot], cluster)
        partner = partner_product(tile, index, gathered_ref, side_ref, rows_ref, grids, 0, (1,))
        new = tile.astype(F32) + sign * (nn(x0, tile) + partner)
        new_ref[slot - 1] = new
        stores[slot - 1].start()
        rounded = new.astype(BF).astype(F32)
        squares += rounded * rounded
    row, col = index_grids(size)
    trace = jnp.sum(jnp.where(row == col, diag - 0.25 * next_sign, 0.0) + next_sign * squares)
    lane = lax.broadcasted_iota(jnp.int32, (1, h), 1)
    left = jnp.full((1, h), trace, F32)
    line = jnp.zeros((1, h), F32)
    for k in range(3):
        piece = left.astype(BF).astype(F32)
        line = jnp.where(lane == k, piece, line)
        left = left - piece
    last = sent_ref.shape[1] - 1
    at = lax.broadcasted_iota(jnp.int32, (last + 1, h), 0)
    sent_ref[0] = jnp.where(at == last, line, held_ref[...].astype(F32)).astype(BF)
    for store in stores:
        store.wait()


def third_kernel(
    cluster, branch_ref, cols_ref, diag_ref, new_hbm, gathered_ref, side_ref,
    out_hbm, occupation_ref, new_ref, out_ref, rows_ref, load_sems, store_sems,
):
    tiles, size = out_ref.shape[:2]
    loads = [pltpu.make_async_copy(new_hbm.at[s], new_ref.at[s], load_sems.at[s]) for s in range(tiles - 1)]
    stores = [pltpu.make_async_copy(out_ref.at[s], out_hbm.at[s], store_sems.at[s]) for s in range(tiles)]
    for load in loads:
        load.start()
    sign = sign_of(branch_ref, 1)
    grids = index_grids(size // 2)
    last = gathered_ref.shape[1] - 1
    lines = jnp.zeros((1, size // 2), F32)
    for member in range(cluster):
        lines += gathered_ref[member].astype(F32)[last:]
    occupation_ref[0] = jnp.sum(lines) / (cluster * size) + 0.5
    diag = diag_ref[...]
    r0 = diag.astype(BF)
    total = nt(r0, r0)
    for slot in range(1, tiles):
        loads[slot - 1].wait()
        new = new_ref[slot - 1]
        r = new.astype(BF)
        total += nt(r, r)
        index = lax.rem(cols_ref[0, slot], cluster)
        partner = partner_product(r, index, gathered_ref, side_ref, rows_ref, grids, 2, (3, 4))
        out_ref[slot] = new + sign * (nn(r0, r) + partner)
        stores[slot].start()
    out_ref[0] = diag + sign * (total - quarter_identity(size))
    stores[0].start()
    for store in stores:
        store.wait()


S, V, A = (pl.BlockSpec(memory_space=m) for m in (pltpu.SMEM, pltpu.VMEM, pl.ANY))


def call(kernel, ins, outs, scratch, args, name):
    return pl.pallas_call(
        kernel,
        out_shape=[jax.ShapeDtypeStruct(shape, dtype) for shape, dtype, _ in outs],
        in_specs=list(ins),
        out_specs=[spec for _, _, spec in outs],
        scratch_shapes=scratch,
        compiler_params=pltpu.CompilerParams(vmem_limit_bytes=24 * 1024 * 1024),
        name=name,
    )(*args)


def shards(x_tiles, columns, branch):
    tiles, size = x_tiles.shape[1], x_tiles.shape[2]
    h = size // 2
    cluster = x_tiles.shape[0] * lax.axis_size("col")
    x = x_tiles.reshape(tiles, size, size)
    sems = pltpu.SemaphoreType.DMA((tiles,))
    many = pltpu.VMEM((tiles, size, size), BF)
    fewer = (tiles - 1, size, size)

    sent0, side, held, diag = call(
        first_kernel,
        (S, A),
        [((1, size - 1, h), BF, V), ((cluster, SIDE_ROWS, h), BF, V), ((size - 1, h), BF, V), ((size, size), F32, V)],
        [many, sems],
        (branch, x),
        "first",
    )
    sides = lax.all_to_all(side, "col", 0, 0, tiled=True)
    gathered0 = lax.all_gather(sent0, "col", axis=0, tiled=True)
    new, sent1 = call(
        lambda *refs: second_kernel(cluster, *refs),
        (S, S, A, V, V, V, V),
        [(fewer, F32, A), ((1, size - 1, h), BF, V)],
        [many, pltpu.VMEM(fewer, F32), pltpu.VMEM((size, h), F32), sems, sems],
        (branch, columns, x, diag, held, gathered0, sides),
        "second",
    )
    gathered1 = lax.all_gather(sent1, "col", axis=0, tiled=True)
    out, occupation = call(
        lambda *refs: third_kernel(cluster, *refs),
        (S, S, V, A, V, V),
        [((tiles, size, size), F32, A), ((1,), F32, S)],
        [pltpu.VMEM(fewer, F32), pltpu.VMEM((tiles, size, size), F32), pltpu.VMEM((size, h), F32), sems, sems],
        (branch, columns, diag, new, gathered1, sides),
        "third",
    )
    return out.reshape(x_tiles.shape), occupation


def solution(mesh):
    placed = (P(("row", "col"), None, None, None), P(("row", "col"), None), P("row", None))
    return jax.shard_map(
        shards,
        mesh=mesh,
        in_specs=placed,
        out_specs=(P(("row", "col"), None, None, None), P("row")),
        check_vma=False,
    )
```

```python
import jax
import jax.numpy as jnp
from jax import lax
from jax.experimental import pallas as pl
from jax.experimental.pallas import tpu as pltpu
from jax.sharding import PartitionSpec as P

BF = jnp.bfloat16
F32 = jnp.float32

def nt(a, b):
    return lax.dot_general(a, b, (((1,), (1,)), ((), ())), preferred_element_type=F32)


def nn(a, b):
    return jnp.dot(a, b, preferred_element_type=F32)


def index_grids(h):
    return (lax.broadcasted_iota(jnp.int32, (h, h), 0), lax.broadcasted_iota(jnp.int32, (h, h), 1))


def quarter_identity(size):
    row, col = index_grids(size)
    return jnp.where(row == col, 0.25, 0.0).astype(F32)


def sign_of(branch_ref, step):
    return (2 * branch_ref[0, step] - 1).astype(F32)


def mixed_part(tile):
    h = tile.shape[0] // 2
    row, col = index_grids(h)
    return jnp.where(row <= col, tile[:h, :h], pltpu.roll(tile[h:, h:], 1, 0))


def symmetric_product(tile, mixed, below, c_last, grids):
    row, col = grids
    h = mixed.shape[0]
    c = jnp.where(row == h - 1, c_last, pltpu.roll(mixed, h - 1, 0))
    zero = jnp.zeros_like(mixed)
    stack = lambda a, b, d: jnp.concatenate(
        [jnp.concatenate([a, zero], axis=1), jnp.concatenate([b, d], axis=1)], axis=0
    ).astype(BF)
    straight = stack(jnp.where(row <= col, mixed, 0.0), below, jnp.where(row >= col, c, 0.0))
    flipped = stack(jnp.where(row < col, mixed, 0.0), below, jnp.where(row > col, c, 0.0))
    return (nn(tile, straight) + nt(tile, flipped)).astype(BF).astype(F32)


SIDE_ROWS = 8


def first_kernel(branch_hbm, x_hbm, sent0_ref, side_ref, held_ref, diag_ref, x_ref, rows_ref, branch_ref, sems, branch_sem):
    tiles, size = x_ref.shape[:2]
    h = size // 2
    loads = [pltpu.make_async_copy(x_hbm.at[s], x_ref.at[s], sems.at[s]) for s in range(tiles)]
    scalars = pltpu.make_async_copy(branch_hbm, branch_ref, branch_sem)
    for load in loads:
        load.start()
    scalars.start()
    loads[0].wait()
    x0 = x_ref[0]
    old = x0.astype(F32)
    sent0_ref[0, :h] = mixed_part(old).astype(BF)
    sent0_ref[0, h:] = x0[h : size - 1, :h]
    total = nt(x0, x0)
    for slot in range(1, tiles):
        loads[slot].wait()
        total += nt(x_ref[slot], x_ref[slot])
    scalars.wait()
    new = old + sign_of(branch_ref, 0) * (total - quarter_identity(size))
    diag_ref[...] = new
    held_ref[:h] = mixed_part(new).astype(BF)
    held_ref[h:] = new[h : size - 1, :h].astype(BF)
    rows_ref[...] = jnp.zeros(rows_ref.shape, F32)
    rows_ref[0:1] = old[size - 1 :, :h]
    rows_ref[1:2] = old[size - 1 :, h:]
    rows_ref[2:3] = new[size - 1 :, :h]
    rows_ref[3:4] = new[size - 1 :, h:]
    rows_ref[4:5] = new[size - 2 : size - 1, :h]
    side = rows_ref[...].astype(BF)
    for slot in range(side_ref.shape[0]):
        side_ref[slot] = side


def second_kernel(
    cluster, branch_ref, cols_ref, x_ref, diag_ref, held_ref, gathered_ref, side_ref, new_ref, sent_ref, rows_ref
):
    tiles, size = x_ref.shape[:2]
    h = size // 2
    sign, next_sign = sign_of(branch_ref, 0), sign_of(branch_ref, 1)
    grids = index_grids(h)
    diag = diag_ref[...]
    rounded = diag.astype(BF).astype(F32)
    squares = rounded * rounded
    x0 = x_ref[0]
    for slot in range(1, tiles):
        tile = x_ref[slot]
        partner = lax.rem(cols_ref[0, slot], cluster)
        side = side_ref[partner].astype(F32)
        rows = rows_ref.at[slot % rows_ref.shape[0]]
        rows[: size - 1] = gathered_ref[partner].astype(F32)
        rows[size - 1 :] = side[0:1]
        product = symmetric_product(tile, rows[:h], rows[h:], side[1:2], grids)
        new = tile.astype(F32) + sign * (nn(x0, tile) + product)
        new_ref[slot - 1] = new
        rounded = new.astype(BF).astype(F32)
        squares += rounded * rounded
    row, col = index_grids(size)
    trace = jnp.sum(jnp.where(row == col, diag - 0.25 * next_sign, 0.0) + next_sign * squares)
    lane = lax.broadcasted_iota(jnp.int32, (8, h), 1)
    left = jnp.full((8, h), trace, F32)
    line = jnp.zeros((8, h), F32)
    for k in range(3):
        piece = left.astype(BF).astype(F32)
        line = jnp.where(lane == k, piece, line)
        left = left - piece
    sent_ref[0] = held_ref[...]
    sent_ref[0, size - 2 :] = line[:1].astype(BF)


def third_kernel(
    cluster, branch_ref, cols_ref, diag_ref, new_ref, gathered_ref, side_ref,
    out_hbm, occupation_ref, out_ref, rows_ref, store_sems,
):
    tiles, size = out_ref.shape[:2]
    h = size // 2
    stores = [pltpu.make_async_copy(out_ref.at[s], out_hbm.at[s], store_sems.at[s]) for s in range(tiles)]
    sign = sign_of(branch_ref, 1)
    grids = index_grids(h)
    diag = diag_ref[...]
    r0 = diag.astype(BF)
    total = nt(r0, r0)
    for slot in range(1, tiles):
        new = new_ref[slot - 1]
        r = new.astype(BF)
        total += nt(r, r)
        partner = lax.rem(cols_ref[0, slot], cluster)
        side = side_ref[partner].astype(F32)
        rows = rows_ref.at[slot % rows_ref.shape[0]]
        rows[: size - 1] = gathered_ref[partner].astype(F32)
        rows[size - 2 : size - 1] = side[4:5]
        rows[size - 1 :] = side[2:3]
        product = symmetric_product(r, rows[:h], rows[h:], side[3:4], grids)
        out_ref[slot] = new + sign * (nn(r0, r) + product)
        stores[slot].start()
    out_ref[0] = diag + sign * (total - quarter_identity(size))
    stores[0].start()
    lines = jnp.zeros((1, h), F32)
    for member in range(cluster):
        lines += gathered_ref[member, size - 9 :].astype(F32)[7:]
    occupation_ref[0] = jnp.sum(lines) / (cluster * size) + 0.5
    for store in stores:
        store.wait()


S, V, H = (pl.BlockSpec(memory_space=m) for m in (pltpu.SMEM, pltpu.VMEM, pltpu.HBM))


def call(kernel, ins, outs, scratch, args, name):
    return pl.pallas_call(
        kernel,
        out_shape=[jax.ShapeDtypeStruct(shape, dtype) for shape, dtype, _ in outs],
        in_specs=list(ins),
        out_specs=[spec for _, _, spec in outs],
        scratch_shapes=scratch,
        compiler_params=pltpu.CompilerParams(vmem_limit_bytes=16 * 1024 * 1024),
        name=name,
    )(*args)


def shards(x_tiles, columns, branch):
    tiles, size = x_tiles.shape[1], x_tiles.shape[2]
    h = size // 2
    cluster = x_tiles.shape[0] * lax.axis_size("col")
    x = x_tiles.reshape(tiles, size, size)
    sems = pltpu.SemaphoreType.DMA((tiles,))
    most, rows = (size - 1, h), pltpu.VMEM((2, size, h), F32)

    sent0, side, held, diag = call(
        first_kernel,
        (H, H),
        [((1, *most), BF, V), ((cluster, SIDE_ROWS, h), BF, V), (most, BF, V), ((size, size), F32, V)],
        [
            pltpu.VMEM((tiles, size, size), BF),
            pltpu.VMEM((SIDE_ROWS, h), F32),
            pltpu.SMEM(branch.shape, jnp.int32),
            sems,
            pltpu.SemaphoreType.DMA,
        ],
        (pltpu.with_memory_space_constraint(branch, pltpu.HBM), pltpu.with_memory_space_constraint(x, pltpu.HBM)),
        "first",
    )
    sides = lax.all_to_all(side, "col", 0, 0, tiled=True)
    gathered0 = lax.all_gather(sent0, "col", axis=0, tiled=True)
    new, sent1 = call(
        lambda *refs: second_kernel(cluster, *refs),
        (S, S, V, V, V, V, V),
        [((tiles - 1, size, size), F32, V), ((1, *most), BF, V)],
        [rows],
        (branch, columns, x, diag, held, gathered0, sides),
        "second",
    )
    gathered1 = lax.all_gather(sent1, "col", axis=0, tiled=True)
    out, occupation = call(
        lambda *refs: third_kernel(cluster, *refs),
        (S, S, V, V, V, V),
        [((tiles, size, size), F32, H), ((1,), F32, S)],
        [pltpu.VMEM((tiles, size, size), F32), rows, sems],
        (branch, columns, diag, new, gathered1, sides),
        "third",
    )
    return out.reshape(x_tiles.shape), occupation


def solution(mesh):
    placed = (P(("row", "col"), None, None, None), P(("row", "col"), None), P("row", None))
    return jax.shard_map(
        shards,
        mesh=mesh,
        in_specs=placed,
        out_specs=(P(("row", "col"), None, None, None), P("row")),
        check_vma=False,
    )
```

```python
import jax
import jax.numpy as jnp
from jax import lax
from jax.experimental import pallas as pl
from jax.experimental.pallas import tpu as pltpu
from jax.sharding import PartitionSpec as P

BF = jnp.bfloat16
F32 = jnp.float32

def nt(a, b):
    return lax.dot_general(a, b, (((1,), (1,)), ((), ())), preferred_element_type=F32)


def nn(a, b):
    return jnp.dot(a, b, preferred_element_type=F32)


def index_grids(h):
    return (lax.broadcasted_iota(jnp.int32, (h, h), 0), lax.broadcasted_iota(jnp.int32, (h, h), 1))


def quarter_identity(size):
    row, col = index_grids(size)
    return jnp.where(row == col, 0.25, 0.0).astype(F32)


def sign_of(branch_ref, step):
    return (2 * branch_ref[0, step] - 1).astype(F32)


def mixed_part(tile):
    h = tile.shape[0] // 2
    row, col = index_grids(h)
    return jnp.where(row <= col, tile[:h, :h], pltpu.roll(tile[h:, h:], 1, 0))


def symmetric_product(tile, mixed, below, c_last, grids):
    row, col = grids
    h = mixed.shape[0]
    c = jnp.where(row == h - 1, c_last, pltpu.roll(mixed, h - 1, 0))
    above = jnp.concatenate([jnp.where(row <= col, mixed, mixed.T), below.T], axis=1)
    under = jnp.concatenate([below, jnp.where(row >= col, c, c.T)], axis=1)
    return nn(tile, jnp.concatenate([above, under], axis=0).astype(BF)).astype(BF).astype(F32)


SIDE_ROWS = 8


def first_kernel(branch_hbm, x_hbm, sent_ref, diag_ref, x_ref, branch_ref, sems, branch_sem):
    tiles, size = x_ref.shape[:2]
    h = size // 2
    loads = [pltpu.make_async_copy(x_hbm.at[s], x_ref.at[s], sems.at[s]) for s in range(tiles)]
    scalars = pltpu.make_async_copy(branch_hbm, branch_ref, branch_sem)
    for load in loads:
        load.start()
    scalars.start()
    loads[0].wait()
    x0 = x_ref[0]
    old = x0.astype(F32)
    sent_ref[0, :h] = mixed_part(old).astype(BF)
    sent_ref[0, h:size] = x0[h:, :h]
    total = nt(x0, x0)
    for slot in range(1, tiles):
        loads[slot].wait()
        total += nt(x_ref[slot], x_ref[slot])
    scalars.wait()
    new = old + sign_of(branch_ref, 0) * (total - quarter_identity(size))
    diag_ref[...] = new
    sent_ref[0, size : size + h] = mixed_part(new).astype(BF)
    sent_ref[0, size + h : 2 * size - 2] = new[h : size - 2, :h].astype(BF)
    sent_ref[0, 2 * size - 2 :] = old[size - 1 :, h:].astype(BF)


def second_kernel(cluster, branch_ref, cols_ref, x_ref, diag_ref, gathered_ref, new_ref, side_ref, rows_ref):
    tiles, size = x_ref.shape[:2]
    h = size // 2
    sign, next_sign = sign_of(branch_ref, 0), sign_of(branch_ref, 1)
    grids = index_grids(h)
    diag = diag_ref[...]
    rounded = diag.astype(BF).astype(F32)
    squares = rounded * rounded
    x0 = x_ref[0]
    for slot in range(1, tiles):
        tile = x_ref[slot]
        partner = lax.rem(cols_ref[0, slot], cluster // 2)
        rows = gathered_ref[partner, :size].astype(F32)
        c_last = gathered_ref[partner, 2 * size - 8 :].astype(F32)[6:]
        product = symmetric_product(tile, rows[:h], rows[h:], c_last, grids)
        new = tile.astype(F32) + sign * (nn(x0, tile) + product)
        new_ref[slot - 1] = new
        rounded = new.astype(BF).astype(F32)
        squares += rounded * rounded
    row, col = index_grids(size)
    trace = jnp.sum(jnp.where(row == col, diag - 0.25 * next_sign, 0.0) + next_sign * squares)
    lane = lax.broadcasted_iota(jnp.int32, (SIDE_ROWS, h), 1)
    left = jnp.full((SIDE_ROWS, h), trace, F32)
    line = jnp.zeros((SIDE_ROWS, h), F32)
    for k in range(3):
        piece = left.astype(BF).astype(F32)
        line = jnp.where(lane == k, piece, line)
        left = left - piece
    rows_ref[...] = line
    rows_ref[0:1] = diag[size - 2 : size - 1, :h]
    rows_ref[1:2] = diag[size - 1 :, :h]
    rows_ref[2:3] = diag[size - 1 :, h:]
    side = rows_ref[...].astype(BF)
    for slot in range(side_ref.shape[0]):
        side_ref[slot] = side


def third_kernel(
    cluster, branch_ref, cols_ref, diag_ref, new_ref, gathered_ref, side_ref,
    out_hbm, occupation_ref, out_ref, rows_ref, store_sems,
):
    tiles, size = out_ref.shape[:2]
    h = size // 2
    stores = [pltpu.make_async_copy(out_ref.at[s], out_hbm.at[s], store_sems.at[s]) for s in range(tiles)]
    sign = sign_of(branch_ref, 1)
    grids = index_grids(h)
    diag = diag_ref[...]
    r0 = diag.astype(BF)
    total = nt(r0, r0)
    for slot in range(1, tiles):
        new = new_ref[slot - 1]
        r = new.astype(BF)
        total += nt(r, r)
        column = cols_ref[0, slot]
        side = side_ref[lax.rem(column, cluster)].astype(F32)
        rows = rows_ref.at[slot % rows_ref.shape[0]]
        rows[: size - 1] = gathered_ref[lax.rem(column, cluster // 2), size:].astype(F32)
        rows[size - 2 :] = side[0:2]
        product = symmetric_product(r, rows[:h], rows[h:], side[2:3], grids)
        out_ref[slot] = new + sign * (nn(r0, r) + product)
        stores[slot].start()
    out_ref[0] = diag + sign * (total - quarter_identity(size))
    stores[0].start()
    lines = jnp.zeros((SIDE_ROWS, h), F32)
    for member in range(cluster):
        lines += side_ref[member].astype(F32)
    occupation_ref[0] = jnp.sum(lines[3:4]) / (cluster * size) + 0.5
    for store in stores:
        store.wait()


S, V, H = (pl.BlockSpec(memory_space=m) for m in (pltpu.SMEM, pltpu.VMEM, pltpu.HBM))


def call(kernel, ins, outs, scratch, args, name):
    return pl.pallas_call(
        kernel,
        out_shape=[jax.ShapeDtypeStruct(shape, dtype) for shape, dtype, _ in outs],
        in_specs=list(ins),
        out_specs=[spec for _, _, spec in outs],
        scratch_shapes=scratch,
        compiler_params=pltpu.CompilerParams(vmem_limit_bytes=16 * 1024 * 1024),
        name=name,
    )(*args)


def shards(x_tiles, columns, branch):
    tiles, size = x_tiles.shape[1], x_tiles.shape[2]
    h = size // 2
    cluster = x_tiles.shape[0] * lax.axis_size("col")
    x = x_tiles.reshape(tiles, size, size)
    sems = pltpu.SemaphoreType.DMA((tiles,))
    tile32, fewer = (size, size), (tiles - 1, size, size)
    halves = [list(range(cluster // 2)), list(range(cluster // 2, cluster))]
    across = [(i, (i + cluster // 2) % cluster) for i in range(cluster)]

    sent, diag = call(
        first_kernel,
        (H, H),
        [((1, 2 * size - 1, h), BF, V), (tile32, F32, V)],
        [pltpu.VMEM((tiles, size, size), BF), pltpu.SMEM(branch.shape, jnp.int32), sems, pltpu.SemaphoreType.DMA],
        (pltpu.with_memory_space_constraint(branch, pltpu.HBM), pltpu.with_memory_space_constraint(x, pltpu.HBM)),
        "first",
    )
    crossed = lax.ppermute(sent, "col", across)
    gathered = lax.all_gather(crossed, "col", axis=0, tiled=True, axis_index_groups=halves)
    new, side = call(
        lambda *refs: second_kernel(cluster, *refs),
        (S, S, V, V, V),
        [(fewer, F32, V), ((cluster, SIDE_ROWS, h), BF, V)],
        [pltpu.VMEM((SIDE_ROWS, h), F32)],
        (branch, columns, x, diag, gathered),
        "second",
    )
    sides = lax.all_to_all(side, "col", 0, 0, tiled=True)
    out, occupation = call(
        lambda *refs: third_kernel(cluster, *refs),
        (S, S, V, V, V, V),
        [((tiles, size, size), F32, H), ((1,), F32, S)],
        [pltpu.VMEM((tiles, size, size), F32), pltpu.VMEM((2, size, h), F32), sems],
        (branch, columns, diag, new, gathered, sides),
        "third",
    )
    return out.reshape(x_tiles.shape), occupation


def solution(mesh):
    placed = (P(("row", "col"), None, None, None), P(("row", "col"), None), P("row", None))
    return jax.shard_map(
        shards,
        mesh=mesh,
        in_specs=placed,
        out_specs=(P(("row", "col"), None, None, None), P("row")),
        check_vma=False,
    )
```

```python
import jax
import jax.numpy as jnp
from jax import lax
from jax.experimental import pallas as pl
from jax.experimental.pallas import tpu as pltpu
from jax.sharding import PartitionSpec as P

BF = jnp.bfloat16
F32 = jnp.float32

def nt(a, b):
    return lax.dot_general(a, b, (((1,), (1,)), ((), ())), preferred_element_type=F32)


def nn(a, b):
    return jnp.dot(a, b, preferred_element_type=F32)


def index_grids(h):
    return (lax.broadcasted_iota(jnp.int32, (h, h), 0), lax.broadcasted_iota(jnp.int32, (h, h), 1))


def quarter_identity(size):
    row, col = index_grids(size)
    return jnp.where(row == col, 0.25, 0.0).astype(F32)


def sign_of(branch_ref, step):
    return (2 * branch_ref[0, step] - 1).astype(F32)


def mixed_part(tile):
    h = tile.shape[0] // 2
    row, col = index_grids(h)
    return jnp.where(row <= col, tile[:h, :h], pltpu.roll(tile[h:, h:], 1, 0))


def symmetric_product(tile, mixed, below, c_last, grids):
    row, col = grids
    h = mixed.shape[0]
    c = jnp.where(row == h - 1, c_last, pltpu.roll(mixed, h - 1, 0))
    above = jnp.concatenate([jnp.where(row <= col, mixed, mixed.T), below.T], axis=1)
    under = jnp.concatenate([below, jnp.where(row >= col, c, c.T)], axis=1)
    return nn(tile, jnp.concatenate([above, under], axis=0).astype(BF)).astype(BF).astype(F32)


SIDE_ROWS, ASIDE = 16, 8


def holder_of(column, cluster):
    return lax.bitwise_xor(lax.rem(column, cluster // 2), cluster // 4)


def first_kernel(branch_hbm, x_hbm, sent_ref, diag_ref, x_ref, branch_ref, sems, branch_sem):
    tiles, size = x_ref.shape[:2]
    h = size // 2
    loads = [pltpu.make_async_copy(x_hbm.at[s], x_ref.at[s], sems.at[s]) for s in range(tiles)]
    scalars = pltpu.make_async_copy(branch_hbm, branch_ref, branch_sem)
    for load in loads:
        load.start()
    scalars.start()
    loads[0].wait()
    x0 = x_ref[0]
    old = x0.astype(F32)
    sent_ref[0, :h] = mixed_part(old).astype(BF)
    sent_ref[0, h:size] = x0[h:, :h]
    total = None
    for part in (range(tiles // 2), range(tiles // 2, tiles)):
        for slot in part:
            if slot:
                loads[slot].wait()
        wide = jnp.concatenate([x_ref[slot] for slot in part], axis=1)
        total = nt(wide, wide) if total is None else total + nt(wide, wide)
    scalars.wait()
    new = old + sign_of(branch_ref, 0) * (total - quarter_identity(size))
    diag_ref[...] = new
    sent_ref[0, size : size + h] = mixed_part(new).astype(BF)
    sent_ref[0, size + h : 2 * size - ASIDE] = new[h : size - ASIDE, :h].astype(BF)
    sent_ref[0, 2 * size - ASIDE :] = old[size - 1 :, h:].astype(BF)


def second_kernel(cluster, branch_ref, cols_ref, x_ref, diag_ref, gathered_ref, new_ref, side_ref, rows_ref):
    tiles, size = x_ref.shape[:2]
    h = size // 2
    sign, next_sign = sign_of(branch_ref, 0), sign_of(branch_ref, 1)
    grids = index_grids(h)
    diag = diag_ref[...]
    rounded = diag.astype(BF).astype(F32)
    squares = rounded * rounded
    x0 = x_ref[0]
    for slot in range(1, tiles):
        tile = x_ref[slot]
        partner = holder_of(cols_ref[0, slot], cluster)
        rows = gathered_ref[partner, :size].astype(F32)
        c_last = gathered_ref[partner, 2 * size - ASIDE :].astype(F32)
        product = symmetric_product(tile, rows[:h], rows[h:], c_last, grids)
        new = tile.astype(F32) + sign * (nn(x0, tile) + product)
        new_ref[slot - 1] = new
        rounded = new.astype(BF).astype(F32)
        squares += rounded * rounded
    row, col = index_grids(size)
    trace = jnp.sum(jnp.where(row == col, diag - 0.25 * next_sign, 0.0) + next_sign * squares)
    lane = lax.broadcasted_iota(jnp.int32, (SIDE_ROWS, h), 1)
    left = jnp.full((SIDE_ROWS, h), trace, F32)
    line = jnp.zeros((SIDE_ROWS, h), F32)
    for k in range(3):
        piece = left.astype(BF).astype(F32)
        line = jnp.where(lane == k, piece, line)
        left = left - piece
    rows_ref[...] = line
    rows_ref[:ASIDE] = diag[size - ASIDE :, :h]
    rows_ref[ASIDE : ASIDE + 1] = diag[size - 1 :, h:]
    side = rows_ref[...].astype(BF)
    for slot in range(side_ref.shape[0]):
        side_ref[slot] = side


def third_kernel(
    cluster, branch_ref, cols_ref, diag_ref, new_ref, gathered_ref, side_ref,
    out_hbm, occupation_hbm, out_ref, occupation_ref, store_sems, occupation_sem,
):
    tiles, size = out_ref.shape[:2]
    h = size // 2
    stores = [pltpu.make_async_copy(out_ref.at[s], out_hbm.at[s], store_sems.at[s]) for s in range(tiles)]
    lines = jnp.zeros((SIDE_ROWS, h), F32)
    for member in range(cluster):
        lines += side_ref[member].astype(F32)
    occupation_ref[0] = jnp.sum(lines[ASIDE + 1 : ASIDE + 2]) / (cluster * size) + 0.5
    stores.append(pltpu.make_async_copy(occupation_ref, occupation_hbm, occupation_sem))
    stores[tiles].start()
    sign = sign_of(branch_ref, 1)
    grids = index_grids(h)
    diag = diag_ref[...]
    r0 = diag.astype(BF)
    total = nt(r0, r0)
    for slot in range(1, tiles):
        new = new_ref[slot - 1]
        r = new.astype(BF)
        total += nt(r, r)
        column = cols_ref[0, slot]
        side = side_ref[lax.rem(column, cluster)].astype(F32)
        rows = gathered_ref[holder_of(column, cluster), size : 2 * size - ASIDE].astype(F32)
        below = jnp.concatenate([rows[h:], side[:ASIDE]], axis=0)
        product = symmetric_product(r, rows[:h], below, side[ASIDE : ASIDE + 1], grids)
        out_ref[slot] = new + sign * (nn(r0, r) + product)
        stores[slot].start()
    out_ref[0] = diag + sign * (total - quarter_identity(size))
    stores[0].start()
    for store in stores:
        store.wait()


S, V, H = (pl.BlockSpec(memory_space=m) for m in (pltpu.SMEM, pltpu.VMEM, pltpu.HBM))


def call(kernel, ins, outs, scratch, args, name):
    return pl.pallas_call(
        kernel,
        out_shape=[jax.ShapeDtypeStruct(shape, dtype) for shape, dtype, _ in outs],
        in_specs=list(ins),
        out_specs=[spec for _, _, spec in outs],
        scratch_shapes=scratch,
        compiler_params=pltpu.CompilerParams(vmem_limit_bytes=16 * 1024 * 1024),
        name=name,
    )(*args)


def shards(x_tiles, columns, branch):
    tiles, size = x_tiles.shape[1], x_tiles.shape[2]
    h = size // 2
    cluster = x_tiles.shape[0] * lax.axis_size("col")
    x = x_tiles.reshape(tiles, size, size)
    sems = pltpu.SemaphoreType.DMA((tiles,))
    tile32, fewer = (size, size), (tiles - 1, size, size)
    halves = [list(range(cluster // 2)), list(range(cluster // 2, cluster))]
    across = [(i, i ^ (cluster // 2 + cluster // 4)) for i in range(cluster)]

    sent, diag = call(
        first_kernel,
        (H, H),
        [((1, 2 * size - ASIDE + 1, h), BF, V), (tile32, F32, V)],
        [pltpu.VMEM((tiles, size, size), BF), pltpu.SMEM(branch.shape, jnp.int32), sems, pltpu.SemaphoreType.DMA],
        (pltpu.with_memory_space_constraint(branch, pltpu.HBM), pltpu.with_memory_space_constraint(x, pltpu.HBM)),
        "first",
    )
    crossed = lax.ppermute(sent, "col", across)
    gathered = lax.all_gather(crossed, "col", axis=0, tiled=True, axis_index_groups=halves)
    new, side = call(
        lambda *refs: second_kernel(cluster, *refs),
        (S, S, V, V, V),
        [(fewer, F32, V), ((cluster, SIDE_ROWS, h), BF, V)],
        [pltpu.VMEM((SIDE_ROWS, h), F32)],
        (branch, columns, x, diag, gathered),
        "second",
    )
    sides = lax.all_to_all(side, "col", 0, 0, tiled=True)
    out, occupation = call(
        lambda *refs: third_kernel(cluster, *refs),
        (S, S, V, V, V, V),
        [((tiles, size, size), F32, H), ((1,), F32, H)],
        [pltpu.VMEM((tiles, size, size), F32), pltpu.SMEM((1,), F32), sems, pltpu.SemaphoreType.DMA],
        (branch, columns, diag, new, gathered, sides),
        "third",
    )
    return out.reshape(x_tiles.shape), occupation


def solution(mesh):
    placed = (P(("row", "col"), None, None, None), P(("row", "col"), None), P("row", None))
    return jax.shard_map(
        shards,
        mesh=mesh,
        in_specs=placed,
        out_specs=(P(("row", "col"), None, None, None), P("row")),
        check_vma=False,
    )
```

```python
import jax
import jax.numpy as jnp
from jax import lax
from jax.experimental import pallas as pl
from jax.experimental.pallas import tpu as pltpu
from jax.sharding import PartitionSpec as P

BF = jnp.bfloat16
F32 = jnp.float32

def nt(a, b):
    return lax.dot_general(a, b, (((1,), (1,)), ((), ())), preferred_element_type=F32)


def nn(a, b):
    return jnp.dot(a, b, preferred_element_type=F32)


def index_grids(h):
    return (lax.broadcasted_iota(jnp.int32, (h, h), 0), lax.broadcasted_iota(jnp.int32, (h, h), 1))


def quarter_identity(size):
    row, col = index_grids(size)
    return jnp.where(row == col, 0.25, 0.0).astype(F32)


def sign_of(branch_ref, step):
    return (2 * branch_ref[0, step] - 1).astype(F32)


def mixed_part(tile):
    h = tile.shape[0] // 2
    row, col = index_grids(h)
    return jnp.where(row <= col, tile[:h, :h], pltpu.roll(tile[h:, h:], 1, 0))


def unfolded(mixed, below, c_last, grids):
    row, col = grids
    h = mixed.shape[0]
    c = jnp.where(row == h - 1, c_last, pltpu.roll(mixed, h - 1, 0))
    above = jnp.concatenate([jnp.where(row <= col, mixed, mixed.T), below.T], axis=1)
    under = jnp.concatenate([below, jnp.where(row >= col, c, c.T)], axis=1)
    return jnp.concatenate([above, under], axis=0).astype(BF)


SIDE_ROWS, ASIDE, NORMS = 24, 8, 16


def holder_of(column, cluster):
    return lax.bitwise_xor(lax.rem(column, cluster // 2), cluster // 4)


def first_kernel(branch_hbm, x_hbm, sent_ref, diag_ref, x_ref, branch_ref, sems, branch_sem):
    tiles, size = x_ref.shape[:2]
    h = size // 2
    loads = [pltpu.make_async_copy(x_hbm.at[s], x_ref.at[s], sems.at[s]) for s in range(tiles)]
    scalars = pltpu.make_async_copy(branch_hbm, branch_ref, branch_sem)
    for load in loads:
        load.start()
    scalars.start()
    loads[0].wait()
    x0 = x_ref[0]
    old = x0.astype(F32)
    sent_ref[0, :h] = mixed_part(old).astype(BF)
    sent_ref[0, h:size] = x0[h:, :h]
    total = None
    for part in (range(tiles // 2), range(tiles // 2, tiles)):
        for slot in part:
            if slot:
                loads[slot].wait()
        wide = jnp.concatenate([x_ref[slot] for slot in part], axis=1)
        total = nt(wide, wide) if total is None else total + nt(wide, wide)
    scalars.wait()
    new = old + sign_of(branch_ref, 0) * (total - quarter_identity(size))
    diag_ref[...] = new
    sent_ref[0, size : size + h] = mixed_part(new).astype(BF)
    sent_ref[0, size + h : 2 * size - ASIDE] = new[h : size - ASIDE, :h].astype(BF)
    sent_ref[0, 2 * size - ASIDE :] = old[size - 1 :, h:].astype(BF)


def diagonal_trace(diag, sign):
    row, col = index_grids(diag.shape[0])
    rounded = diag.astype(BF).astype(F32)
    return jnp.sum(jnp.where(row == col, diag - 0.25 * sign, 0.0) + sign * rounded * rounded)


def in_pieces(value, shape):
    lane = lax.broadcasted_iota(jnp.int32, shape, 1)
    left, line = jnp.broadcast_to(value, shape).astype(F32), jnp.zeros(shape, F32)
    for k in range(3):
        piece = left.astype(BF).astype(F32)
        line = jnp.where(lane == k, piece, line)
        left = left - piece
    return line


def side_kernel(branch_ref, diag_ref, side_ref, rows_ref):
    size = diag_ref.shape[0]
    h = size // 2
    rows_ref[...] = in_pieces(diagonal_trace(diag_ref[...], sign_of(branch_ref, 1)), rows_ref.shape)
    rows_ref[:ASIDE] = diag_ref[size - ASIDE :, :h]
    rows_ref[ASIDE : ASIDE + 1] = diag_ref[size - 1 :, h:]
    side_ref[0] = rows_ref[...].astype(BF)


def second_kernel(
    cluster, branch_ref, cols_ref, x_ref, gathered_ref, own_ref, crossed_ref, new_ref, side_ref
):
    tiles, size = x_ref.shape[:2]
    h = size // 2
    sign = sign_of(branch_ref, 0)
    grids = index_grids(h)
    x0 = x_ref[0]
    at = lax.broadcasted_iota(jnp.int32, (SIDE_ROWS, h), 0)
    norms = jnp.zeros((SIDE_ROWS, h), F32)
    for slot in range(1, tiles):
        tile = x_ref[slot]
        column = cols_ref[0, slot]
        partner = holder_of(column, cluster)
        rows = gathered_ref[partner, :size].astype(F32)
        c_last = gathered_ref[partner, 2 * size - ASIDE :].astype(F32)
        product = nn(tile, unfolded(rows[:h], rows[h:], c_last, grids))
        new = tile.astype(F32) + sign * (nn(x0, tile) + product)
        new_ref[slot - 1] = new
        squares = new.astype(BF).astype(F32)
        squares = squares * squares
        main = squares[:h, :h] + squares[h:, h:]
        even = 0.5 * (main + main.T) + (squares[:h, h:] + squares[h:, :h].T)
        norms = jnp.where(at == NORMS + lax.rem(column, cluster // 2), jnp.sum(even, axis=0, keepdims=True), norms)
    norms = jnp.sum(norms, axis=1, keepdims=True)
    crossed, own = crossed_ref[0].astype(F32), own_ref[0].astype(F32)
    pair = jnp.sum(jnp.where(at == NORMS - 1, crossed, 0.0)) + jnp.sum(jnp.where(at == NORMS - 1, own, 0.0))
    side = jnp.where(at == NORMS - 1, in_pieces(pair, crossed.shape), crossed)
    side = jnp.where(at >= NORMS, in_pieces(norms, crossed.shape), side).astype(BF)
    for slot in range(side_ref.shape[0]):
        side_ref[slot] = side


def third_kernel(
    cluster, branch_ref, cols_ref, diag_ref, new_ref, gathered_ref, side_ref,
    out_hbm, occupation_hbm, out_ref, occupation_ref, store_sems, occupation_sem,
):
    tiles, size = out_ref.shape[:2]
    h = size // 2
    stores = [pltpu.make_async_copy(out_ref.at[s], out_hbm.at[s], store_sems.at[s]) for s in range(tiles)]
    half = side_ref.shape[0]
    read = [side_ref[member].astype(F32) for member in range(half)]
    pairs = [read[member] + read[member + half // 2] for member in range(half // 2)]
    diagonal = jnp.sum(sum(pairs)[NORMS - 1 : NORMS])
    lane = lax.broadcasted_iota(jnp.int32, (half, h), 1)
    norms = jnp.zeros((half, h), F32)
    for member in range(half):
        norms = jnp.where(lane == member, jnp.sum(read[member][NORMS:], axis=1, keepdims=True), norms)
    norms = jnp.concatenate([norms, jnp.zeros((h - half, h), F32)], axis=0)
    trace = diagonal + sign_of(branch_ref, 1) * jnp.sum(norms + norms.T)
    occupation_ref[0] = trace / (cluster * size) + 0.5
    stores.append(pltpu.make_async_copy(occupation_ref, occupation_hbm, occupation_sem))
    stores[tiles].start()
    sign = sign_of(branch_ref, 1)
    grids = index_grids(h)
    diag = diag_ref[...]
    r0 = diag.astype(BF)
    total = nt(r0, r0)
    for slot in range(1, tiles):
        new = new_ref[slot - 1]
        r = new.astype(BF)
        total += nt(r, r)
        column = cols_ref[0, slot]
        holder = holder_of(column, cluster)
        side = side_ref[holder].astype(F32)
        rows = gathered_ref[holder, size : 2 * size - ASIDE].astype(F32)
        below = jnp.concatenate([rows[h:], side[:ASIDE]], axis=0)
        product = nn(r, unfolded(rows[:h], below, side[ASIDE : ASIDE + 1], grids)).astype(BF).astype(F32)
        out_ref[slot] = new + sign * (nn(r0, r) + product)
        stores[slot].start()
    out_ref[0] = diag + sign * (total - quarter_identity(size))
    stores[0].start()
    for store in stores:
        store.wait()


S, V, H = (pl.BlockSpec(memory_space=m) for m in (pltpu.SMEM, pltpu.VMEM, pltpu.HBM))


def call(kernel, ins, outs, scratch, args, name):
    return pl.pallas_call(
        kernel,
        out_shape=[jax.ShapeDtypeStruct(shape, dtype) for shape, dtype, _ in outs],
        in_specs=list(ins),
        out_specs=[spec for _, _, spec in outs],
        scratch_shapes=scratch,
        compiler_params=pltpu.CompilerParams(vmem_limit_bytes=16 * 1024 * 1024),
        name=name,
    )(*args)


def shards(x_tiles, columns, branch):
    tiles, size = x_tiles.shape[1], x_tiles.shape[2]
    h = size // 2
    cluster = x_tiles.shape[0] * lax.axis_size("col")
    x = x_tiles.reshape(tiles, size, size)
    sems = pltpu.SemaphoreType.DMA((tiles,))
    tile32, fewer = (size, size), (tiles - 1, size, size)
    halves = [list(range(cluster // 2)), list(range(cluster // 2, cluster))]
    across = [(i, i ^ (cluster // 2 + cluster // 4)) for i in range(cluster)]

    sent, diag = call(
        first_kernel,
        (H, H),
        [((1, 2 * size - ASIDE + 1, h), BF, V), (tile32, F32, V)],
        [pltpu.VMEM((tiles, size, size), BF), pltpu.SMEM(branch.shape, jnp.int32), sems, pltpu.SemaphoreType.DMA],
        (pltpu.with_memory_space_constraint(branch, pltpu.HBM), pltpu.with_memory_space_constraint(x, pltpu.HBM)),
        "first",
    )
    crossed = lax.ppermute(sent, "col", across)
    (side,) = call(
        side_kernel, (S, V), [((1, SIDE_ROWS, h), BF, V)], [pltpu.VMEM((SIDE_ROWS, h), F32)], (branch, diag), "side"
    )
    crossed_side = lax.ppermute(side, "col", across)
    gathered = lax.all_gather(crossed, "col", axis=0, tiled=True, axis_index_groups=halves)
    new, sides = call(
        lambda *refs: second_kernel(cluster, *refs),
        (S, S, V, V, V, V),
        [(fewer, F32, V), ((cluster // 2, SIDE_ROWS, h), BF, V)],
        [],
        (branch, columns, x, gathered, side, crossed_side),
        "second",
    )
    sides = lax.all_to_all(sides, "col", 0, 0, tiled=True, axis_index_groups=halves)
    out, occupation = call(
        lambda *refs: third_kernel(cluster, *refs),
        (S, S, V, V, V, V),
        [((tiles, size, size), F32, H), ((1,), F32, H)],
        [pltpu.VMEM((tiles, size, size), F32), pltpu.SMEM((1,), F32), sems, pltpu.SemaphoreType.DMA],
        (branch, columns, diag, new, gathered, sides),
        "third",
    )
    return out.reshape(x_tiles.shape), occupation


def solution(mesh):
    placed = (P(("row", "col"), None, None, None), P(("row", "col"), None), P("row", None))
    return jax.shard_map(
        shards,
        mesh=mesh,
        in_specs=placed,
        out_specs=(P(("row", "col"), None, None, None), P("row")),
        check_vma=False,
    )
```

```python
import jax
import jax.numpy as jnp
from jax import lax
from jax.experimental import pallas as pl
from jax.experimental.pallas import tpu as pltpu
from jax.sharding import PartitionSpec as P

BF = jnp.bfloat16
F32 = jnp.float32

def nt(a, b):
    return lax.dot_general(a, b, (((1,), (1,)), ((), ())), preferred_element_type=F32)


def nn(a, b):
    return jnp.dot(a, b, preferred_element_type=F32)


def index_grids(h):
    return (lax.broadcasted_iota(jnp.int32, (h, h), 0), lax.broadcasted_iota(jnp.int32, (h, h), 1))


def quarter_identity(size):
    row, col = index_grids(size)
    return jnp.where(row == col, 0.25, 0.0).astype(F32)


def sign_of(branch_ref, step):
    return (2 * branch_ref[0, step] - 1).astype(F32)


def mixed_part(tile):
    h = tile.shape[0] // 2
    row, col = index_grids(h)
    return jnp.where(row <= col, tile[:h, :h], pltpu.roll(tile[h:, h:], 1, 0))


def unfolded(mixed, below, c_last, grids):
    row, col = grids
    h = mixed.shape[0]
    c = jnp.where(row == h - 1, c_last, pltpu.roll(mixed, h - 1, 0))
    above = jnp.concatenate([jnp.where(row <= col, mixed, mixed.T), below.T], axis=1)
    under = jnp.concatenate([below, jnp.where(row >= col, c, c.T)], axis=1)
    return jnp.concatenate([above, under], axis=0).astype(BF)


SIDE_ROWS, ASIDE, PIECES = 16, 8, 9


def holder_of(column, cluster):
    return lax.bitwise_xor(lax.rem(column, cluster // 2), cluster // 4)


def first_kernel(branch_hbm, x_hbm, sent_ref, diag_ref, x_ref, branch_ref, sems, branch_sem):
    tiles, size = x_ref.shape[:2]
    h = size // 2
    loads = [pltpu.make_async_copy(x_hbm.at[s], x_ref.at[s], sems.at[s]) for s in range(tiles)]
    scalars = pltpu.make_async_copy(branch_hbm, branch_ref, branch_sem)
    for load in loads:
        load.start()
    scalars.start()
    loads[0].wait()
    x0 = x_ref[0]
    old = x0.astype(F32)
    sent_ref[0, :h] = mixed_part(old).astype(BF)
    sent_ref[0, h:size] = x0[h:, :h]
    total = None
    for part in (range(tiles // 2), range(tiles // 2, tiles)):
        for slot in part:
            if slot:
                loads[slot].wait()
        wide = jnp.concatenate([x_ref[slot] for slot in part], axis=1)
        total = nt(wide, wide) if total is None else total + nt(wide, wide)
    scalars.wait()
    new = old + sign_of(branch_ref, 0) * (total - quarter_identity(size))
    diag_ref[...] = new
    sent_ref[0, size : size + h] = mixed_part(new).astype(BF)
    sent_ref[0, size + h : 2 * size - ASIDE] = new[h : size - ASIDE, :h].astype(BF)
    sent_ref[0, 2 * size - ASIDE :] = old[size - 1 :, h:].astype(BF)


def diagonal_trace(diag, sign):
    row, col = index_grids(diag.shape[0])
    rounded = diag.astype(BF).astype(F32)
    return jnp.sum(jnp.where(row == col, diag - 0.25 * sign, 0.0) + sign * rounded * rounded)


def in_pieces(value, shape):
    lane = lax.broadcasted_iota(jnp.int32, shape, 1)
    left, line = jnp.broadcast_to(value, shape).astype(F32), jnp.zeros(shape, F32)
    for k in range(3):
        piece = left.astype(BF).astype(F32)
        line = jnp.where(lane == k, piece, line)
        left = left - piece
    return line


def side_kernel(branch_ref, diag_ref, side_ref, rows_ref):
    size = diag_ref.shape[0]
    h = size // 2
    rows_ref[...] = in_pieces(diagonal_trace(diag_ref[...], sign_of(branch_ref, 1)), rows_ref.shape)
    rows_ref[:ASIDE] = diag_ref[size - ASIDE :, :h]
    rows_ref[ASIDE : ASIDE + 1] = diag_ref[size - 1 :, h:]
    side_ref[0] = rows_ref[...].astype(BF)


def second_kernel(
    cluster, branch_ref, cols_ref, x_ref, gathered_ref, own_ref, crossed_ref, new_ref, side_ref
):
    tiles, size = x_ref.shape[:2]
    h = size // 2
    sign = sign_of(branch_ref, 0)
    grids = index_grids(h)
    x0 = x_ref[0]
    at = lax.broadcasted_iota(jnp.int32, (SIDE_ROWS, h), 0)
    lane = lax.broadcasted_iota(jnp.int32, (SIDE_ROWS, h), 1)
    sums = jnp.zeros((SIDE_ROWS, h), F32)
    for slot in range(1, tiles):
        tile = x_ref[slot]
        column = cols_ref[0, slot]
        partner = holder_of(column, cluster)
        rows = gathered_ref[partner, :size].astype(F32)
        c_last = gathered_ref[partner, 2 * size - ASIDE :].astype(F32)
        product = nn(tile, unfolded(rows[:h], rows[h:], c_last, grids))
        new = tile.astype(F32) + sign * (nn(x0, tile) + product)
        new_ref[slot - 1] = new
        squares = new.astype(BF).astype(F32)
        squares = squares * squares
        main = squares[:h, :h] + squares[h:, h:]
        even = 0.5 * (main + main.T) + (squares[:h, h:] + squares[h:, :h].T)
        norm = jnp.sum(jnp.sum(even, axis=0, keepdims=True), axis=1, keepdims=True)
        sums = jnp.where(lane == lax.rem(column, cluster // 2), norm, sums)
    crossed, own = crossed_ref[0].astype(F32), own_ref[0].astype(F32)
    pair = jnp.sum(jnp.where(at == PIECES, crossed, 0.0)) + jnp.sum(jnp.where(at == PIECES, own, 0.0))
    left, side = jnp.where(lane == cluster // 2, pair, sums), crossed
    for k in range(3):
        piece = left.astype(BF).astype(F32)
        side = jnp.where(at == PIECES + k, piece, side)
        left = left - piece
    side = side.astype(BF)
    for slot in range(side_ref.shape[0]):
        side_ref[slot] = side


def third_kernel(
    cluster, branch_ref, cols_ref, diag_ref, new_ref, gathered_ref, side_ref,
    out_hbm, occupation_hbm, out_ref, occupation_ref, store_sems, occupation_sem,
):
    tiles, size = out_ref.shape[:2]
    h = size // 2
    stores = [pltpu.make_async_copy(out_ref.at[s], out_hbm.at[s], store_sems.at[s]) for s in range(tiles)]
    half = side_ref.shape[0]
    read = [side_ref[member].astype(F32) for member in range(half)]
    lines = [r[PIECES : PIECES + 1] + r[PIECES + 1 : PIECES + 2] + r[PIECES + 2 : PIECES + 3] for r in read]
    pairs = sum(lines[member] + lines[member + half // 2] for member in range(half // 2))
    lane = lax.broadcasted_iota(jnp.int32, (half, h), 1)
    diagonal = jnp.sum(jnp.where(lane[:1] == half, pairs, 0.0))
    at = lax.broadcasted_iota(jnp.int32, (half, h), 0)
    norms = jnp.zeros((half, h), F32)
    for member in range(half):
        norms = jnp.where(at == member, lines[member], norms)
    norms = jnp.where(lane < half, norms, 0.0)
    norms = jnp.concatenate([norms, jnp.zeros((h - half, h), F32)], axis=0)
    trace = diagonal + sign_of(branch_ref, 1) * jnp.sum(norms + norms.T)
    occupation_ref[0] = trace / (cluster * size) + 0.5
    stores.append(pltpu.make_async_copy(occupation_ref, occupation_hbm, occupation_sem))
    stores[tiles].start()
    sign = sign_of(branch_ref, 1)
    grids = index_grids(h)
    diag = diag_ref[...]
    r0 = diag.astype(BF)
    total = nt(r0, r0)
    for slot in range(1, tiles):
        new = new_ref[slot - 1]
        r = new.astype(BF)
        total += nt(r, r)
        column = cols_ref[0, slot]
        holder = holder_of(column, cluster)
        side = side_ref[holder].astype(F32)
        rows = gathered_ref[holder, size : 2 * size - ASIDE].astype(F32)
        below = jnp.concatenate([rows[h:], side[:ASIDE]], axis=0)
        product = nn(r, unfolded(rows[:h], below, side[ASIDE : ASIDE + 1], grids)).astype(BF).astype(F32)
        out_ref[slot] = new + sign * (nn(r0, r) + product)
        stores[slot].start()
    out_ref[0] = diag + sign * (total - quarter_identity(size))
    stores[0].start()
    for store in stores:
        store.wait()


S, V, H = (pl.BlockSpec(memory_space=m) for m in (pltpu.SMEM, pltpu.VMEM, pltpu.HBM))


def call(kernel, ins, outs, scratch, args, name):
    return pl.pallas_call(
        kernel,
        out_shape=[jax.ShapeDtypeStruct(shape, dtype) for shape, dtype, _ in outs],
        in_specs=list(ins),
        out_specs=[spec for _, _, spec in outs],
        scratch_shapes=scratch,
        compiler_params=pltpu.CompilerParams(vmem_limit_bytes=16 * 1024 * 1024),
        name=name,
    )(*args)


def shards(x_tiles, columns, branch):
    tiles, size = x_tiles.shape[1], x_tiles.shape[2]
    h = size // 2
    cluster = x_tiles.shape[0] * lax.axis_size("col")
    x = x_tiles.reshape(tiles, size, size)
    sems = pltpu.SemaphoreType.DMA((tiles,))
    tile32, fewer = (size, size), (tiles - 1, size, size)
    halves = [list(range(cluster // 2)), list(range(cluster // 2, cluster))]
    across = [(i, i ^ (cluster // 2 + cluster // 4)) for i in range(cluster)]

    sent, diag = call(
        first_kernel,
        (H, H),
        [((1, 2 * size - ASIDE + 1, h), BF, V), (tile32, F32, V)],
        [pltpu.VMEM((tiles, size, size), BF), pltpu.SMEM(branch.shape, jnp.int32), sems, pltpu.SemaphoreType.DMA],
        (pltpu.with_memory_space_constraint(branch, pltpu.HBM), pltpu.with_memory_space_constraint(x, pltpu.HBM)),
        "first",
    )
    crossed = lax.ppermute(sent, "col", across)
    (side,) = call(
        side_kernel, (S, V), [((1, SIDE_ROWS, h), BF, V)], [pltpu.VMEM((SIDE_ROWS, h), F32)], (branch, diag), "side"
    )
    crossed_side = lax.ppermute(side, "col", across)
    gathered = lax.all_gather(crossed, "col", axis=0, tiled=True, axis_index_groups=halves)
    new, sides = call(
        lambda *refs: second_kernel(cluster, *refs),
        (S, S, V, V, V, V),
        [(fewer, F32, V), ((cluster // 2, SIDE_ROWS, h), BF, V)],
        [],
        (branch, columns, x, gathered, side, crossed_side),
        "second",
    )
    sides = lax.all_to_all(sides, "col", 0, 0, tiled=True, axis_index_groups=halves)
    out, occupation = call(
        lambda *refs: third_kernel(cluster, *refs),
        (S, S, V, V, V, V),
        [((tiles, size, size), F32, H), ((1,), F32, H)],
        [pltpu.VMEM((tiles, size, size), F32), pltpu.SMEM((1,), F32), sems, pltpu.SemaphoreType.DMA],
        (branch, columns, diag, new, gathered, sides),
        "third",
    )
    return out.reshape(x_tiles.shape), occupation


def solution(mesh):
    placed = (P(("row", "col"), None, None, None), P(("row", "col"), None), P("row", None))
    return jax.shard_map(
        shards,
        mesh=mesh,
        in_specs=placed,
        out_specs=(P(("row", "col"), None, None, None), P("row")),
        check_vma=False,
    )
```
